32 devices in a mesh: outer: 8 (over y, x, core), inner: 4 (over z).
Axes of the slice: x: 2, y: 2, z: 4, core: 2. Of those that a mesh axis runs over, the one named last changes fastest.
Arguments:
- query_image: bfloat16 [2048, 1024], P(('outer', 'inner')), may hold values from -6 to 6
- key_image: bfloat16 [2048, 1024], P(('outer', 'inner')), may hold values from -6 to 6
- value_image: bfloat16 [2048, 1024], P(('outer', 'inner')), may hold values from -6 to 6
- attended_image: bfloat16 [2048, 1024], P(('outer', 'inner')), may hold values from -6 to 6
- upstream_image: bfloat16 [2048, 1024], P(('outer', 'inner')), may hold values from -128 to 128
- logsum_image: float32 [2048, 8], P(('outer', 'inner')), may hold values from 8.6 to 9.4
- query_text: bfloat16 [512, 1024], P(None, 'outer'), may hold values from -6 to 6
- key_text: bfloat16 [512, 1024], P(None, 'outer'), may hold values from -6 to 6
- value_text: bfloat16 [512, 1024], P(None, 'outer'), may hold values from -6 to 6
- attended_text: bfloat16 [512, 1024], P(None, 'outer'), may hold values from -6 to 6
- upstream_text: bfloat16 [512, 1024], P(None, 'outer'), may hold values from -128 to 128
- logsum_text: float32 [512, 8], P(None, 'outer'), may hold values from 8.6 to 9.4
Outputs:
- grad_query_image: bfloat16 [2048, 1024], P(('outer', 'inner'))
- grad_key_image: bfloat16 [2048, 1024], P(('outer', 'inner'))
- grad_value_image: bfloat16 [2048, 1024], P(('outer', 'inner'))
- grad_query_text: bfloat16 [512, 1024], P('inner', 'outer')
- grad_key_text: bfloat16 [512, 1024], P('inner', 'outer')
- grad_value_text: bfloat16 [512, 1024], P('inner', 'outer')
The draws below stay inside these ranges and needn't reach their ends.
All inputs are finite; a program needn't handle non-finite values.
Results may differ from the reference program's by a relative error of at most 0.0055.
Values may be sent and summed in bfloat16 or wider, within the bound.
A program may use at most 64 MiB of HBM per device.

```python
import jax
import jax.numpy as jnp
from jax import lax

HEAD_DIM = 128
TEXT = 512
TOK_DEV = 512
HEADS = 8
IMAGE = 2048
WIDTH = 1024
N_INNER = 4


def block_scale(stream_key, extent, cuts, low, top_value):
    gain, own = 1.0, jax.random.fold_in(stream_key, 6)
    for dim, blocks in cuts:
        steps = jnp.exp(jax.random.uniform(jax.random.fold_in(own, dim), (blocks,), jnp.float32, low / len(cuts), top_value / len(cuts)))
        gain = gain * jnp.repeat(steps, extent[dim] // blocks).reshape([-1 if axis == dim else 1 for axis in range(len(extent))])
    return gain


def scatter_about(rng, shape, spread, bound, pieces=(), kind=jnp.bfloat16):
    values = jax.random.normal(rng, shape, jnp.float32) * spread
    if len(pieces) > 0:
        values = block_scale(rng, shape, pieces, -0.22, 0.18) * values
    return jnp.clip(values, min=-bound, max=bound).astype(kind)


def setup_inputs(seed: int = 0) -> dict:
    key_of = jax.random.split(jax.random.key(seed), 13)
    return {
        "query_image": scatter_about(key_of[0], (IMAGE, WIDTH), 1.0, 6.0, ((0, 32),)),
        "key_image": scatter_about(key_of[1], (IMAGE, WIDTH), 1.0, 6.0, ((0, 32),)),
        "value_image": scatter_about(key_of[2], (IMAGE, WIDTH), 1.0, 6.0, ((0, 32),)),
        "attended_image": scatter_about(key_of[3], (IMAGE, WIDTH), 1.0, 6.0, ((0, 32),)),
        "upstream_image": scatter_about(key_of[4], (IMAGE, WIDTH), 24.0, 128.0, ((0, 32),)),
        "logsum_image": jnp.clip(8.6 + 0.79999924 * jax.random.uniform(key_of[5], (IMAGE, HEADS), jnp.float32) ** block_scale(key_of[5], (IMAGE, HEADS), ((0, 32),), -0.2, 0.2), 8.6, 9.4),
        "query_text": scatter_about(key_of[6], (TEXT, WIDTH), 1.0, 6.0, ((1, 8),)),
        "key_text": scatter_about(key_of[7], (TEXT, WIDTH), 1.0, 6.0, ((1, 8),)),
        "value_text": scatter_about(key_of[8], (TEXT, WIDTH), 1.0, 6.0, ((1, 8),)),
        "attended_text": scatter_about(key_of[9], (TEXT, WIDTH), 1.0, 6.0, ((1, 8),)),
        "upstream_text": scatter_about(key_of[10], (TEXT, WIDTH), 24.0, 128.0, ((1, 8),)),
        "logsum_text": jnp.clip(8.6 + 0.79999924 * jax.random.uniform(key_of[11], (TEXT, HEADS), jnp.float32) ** block_scale(key_of[11], (TEXT, HEADS), ((1, 8),), -0.2, 0.2), 8.6, 9.4),
    }


def weights_and_mixed(queries, upstream, log_sums, deltas, keys, values):
    scores = jnp.dot(queries, keys.T, preferred_element_type=jnp.float32) * (HEAD_DIM ** -0.5)
    weights = jnp.exp(scores - log_sums)
    slopes = jnp.dot(upstream, values.T, preferred_element_type=jnp.float32)
    mixed = weights * (slopes - deltas)
    return weights.astype(jnp.bfloat16), mixed.astype(jnp.bfloat16)


def query_side(mixed_half, keys):
    return jnp.dot(mixed_half, keys, preferred_element_type=jnp.float32) * (HEAD_DIM ** -0.5)


def key_side(weights_half, mixed_half, queries, upstream):
    grad_values = jnp.dot(weights_half.T, upstream, preferred_element_type=jnp.float32)
    grad_keys = jnp.dot(mixed_half.T, queries, preferred_element_type=jnp.float32) * (HEAD_DIM ** -0.5)
    return grad_keys, grad_values


def reference(query_image, key_image, value_image, attended_image, upstream_image, logsum_image,
              query_text, key_text, value_text, attended_text, upstream_text, logsum_text):
    queries = jnp.concatenate([query_text, query_image], axis=0)
    keys = jnp.concatenate([key_text, key_image], axis=0)
    values = jnp.concatenate([value_text, value_image], axis=0)
    attended = jnp.concatenate([attended_text, attended_image], axis=0)
    upstream = jnp.concatenate([upstream_text, upstream_image], axis=0)
    log_sums = jnp.concatenate([logsum_text, logsum_image], axis=0)
    total = TEXT + IMAGE

    def one_head(head):
        start = head * HEAD_DIM

        def columns(matrix):
            return lax.dynamic_slice_in_dim(matrix, start, HEAD_DIM, 1)

        head_q = columns(queries)
        head_k = columns(keys)
        head_v = columns(values)
        head_g = columns(upstream)
        head_o = columns(attended)
        head_l = lax.dynamic_slice_in_dim(log_sums, head, 1, 1)
        head_delta = jnp.sum(head_g.astype(jnp.float32) * head_o.astype(jnp.float32), axis=1, keepdims=True)
        empty = jnp.zeros((total, HEAD_DIM), jnp.float32)

        def block_back(carry, block):
            block_q, block_g, block_l, block_d = block
            weights_half, mixed_half = weights_and_mixed(block_q, block_g, block_l, block_d, head_k, head_v)
            grad_q = query_side(mixed_half, head_k)
            grad_k, grad_v = key_side(weights_half, mixed_half, block_q, block_g)
            return (carry[0] + grad_k, carry[1] + grad_v), grad_q

        carry, text_q = block_back((empty, empty), (head_q[:TEXT], head_g[:TEXT], head_l[:TEXT], head_delta[:TEXT]))
        blocks = tuple(item[TEXT:].reshape((N_INNER, TOK_DEV) + item.shape[1:])
                       for item in (head_q, head_g, head_l, head_delta))
        (grad_k, grad_v), image_q = lax.scan(block_back, carry, blocks)
        grad_q = jnp.concatenate([text_q, image_q.reshape(IMAGE, HEAD_DIM)], axis=0)
        return grad_q, grad_k, grad_v

    grad_q, grad_k, grad_v = lax.map(one_head, jnp.arange(HEADS, dtype=jnp.int32))

    def join_heads(stacked):
        return jnp.transpose(stacked, (1, 0, 2)).reshape(total, HEADS * HEAD_DIM).astype(jnp.bfloat16)

    grad_q = join_heads(grad_q)
    grad_k = join_heads(grad_k)
    grad_v = join_heads(grad_v)
    return (grad_q[TEXT:], grad_k[TEXT:], grad_v[TEXT:],
            grad_q[:TEXT], grad_k[:TEXT], grad_v[:TEXT])
```

```python
import functools
import math

import jax
import jax.numpy as jnp
from jax import lax
from jax.experimental import pallas as pl
from jax.experimental.pallas import tpu as pltpu
from jax.sharding import PartitionSpec as P

HEAD_DIM = 128
LANES = 128
SNAKE = True
MESH = pl.DeviceIdType.MESH


def across_rows(left, right, **options):
    return lax.dot_general(
        left, right, (((1,), (1,)), ((), ())), preferred_element_type=jnp.float32, **options
    )


def kernel(
    dims,
    q_ref, k_ref, v_ref, o_ref, g_ref, l_ref,
    qt_ref, kt_ref, vt_ref, ot_ref, gt_ref, lt_ref,
    out_q, out_k, out_v, out_qt, out_kt, out_vt,
    qg, kv, key_flip, stat_send, stat, row_stat, own_o, own_g, text_o,
    dq_acc, dkv_acc, dq_send, dq_recv, dkv_send, dkv_recv, final,
    local_sem, text_sem, in_send, in_recv, gather_send, gather_recv,
    sum_send, sum_recv, out_send, out_recv,
):
    n_out, n_in, rows, columns, tokens, block, share = dims
    d = HEAD_DIM
    scale = HEAD_DIM ** (-0.5)
    o = lax.axis_index("outer")
    i = lax.axis_index("inner")

    def column_in(row, place):
        if not SNAKE:
            return place
        return place + (row % 2) * (columns - 1 - 2 * place)

    row = i // columns
    column = column_in(row, i % columns)

    def inner_of(row, column):
        return row * columns + column_in(row, column)

    def row_peer(a):
        return inner_of(row, (column + a) % columns)

    def column_peer(b):
        return inner_of((row + b) % rows, column)

    def other(k):
        return (o + k) % n_out

    own_loads = [
        pltpu.make_async_copy(g_ref, own_g, local_sem.at[0]),
        pltpu.make_async_copy(o_ref, own_o, local_sem.at[1]),
    ]
    for copy in own_loads:
        copy.start()

    barrier = pltpu.get_barrier_semaphore()
    for k in range(1, n_out):
        pl.semaphore_signal(barrier, inc=1, device_id=(other(k), i), device_id_type=MESH)
    for a in range(1, columns):
        pl.semaphore_signal(barrier, inc=1, device_id=(o, row_peer(a)), device_id_type=MESH)
    for b in range(1, rows):
        pl.semaphore_signal(barrier, inc=1, device_id=(o, column_peer(b)), device_id_type=MESH)

    text_loads = []

    def text_load(source, peer, target):
        copy = pltpu.make_async_copy(
            source.at[pl.ds(pl.multiple_of(peer * share, share), share)],
            target,
            text_sem.at[len(text_loads)],
        )
        copy.start()
        text_loads.append(copy)

    text = pl.ds(block, share)
    for b in range(rows):
        text_load(kt_ref, column_peer(b), kv.at[b, 0, text])
        text_load(vt_ref, column_peer(b), kv.at[b, 1, text])
    for a in range(columns):
        text_load(qt_ref, row_peer(a), qg.at[a, 0, text])
        text_load(gt_ref, row_peer(a), qg.at[a, 1, text])
        text_load(ot_ref, row_peer(a), text_o.at[a])

    pl.semaphore_wait(barrier, n_out - 1 + columns - 1 + rows - 1)

    own_rows = pl.ds(pl.multiple_of(o * tokens, tokens), tokens)

    def exchange(which, source, target, k):
        if k == 0:
            return pltpu.make_async_copy(source, target, in_recv.at[which, 0])
        return pltpu.make_async_remote_copy(
            src_ref=source,
            dst_ref=target,
            send_sem=in_send.at[which, k],
            recv_sem=in_recv.at[which, k],
            device_id=(other(k), i),
            device_id_type=MESH,
        )

    def head_of(ref, k):
        return ref.at[:, pl.ds(pl.multiple_of(other(k) * d, d), d)]

    homes = (kv.at[0, 0, own_rows], kv.at[0, 1, own_rows], qg.at[0, 0, own_rows], qg.at[0, 1, own_rows])
    arrivals = []
    for pair in ((0, 1), (2, 3)):
        for k in range(n_out):
            for which in pair:
                source = (k_ref, v_ref, q_ref, g_ref)[which]
                copy = exchange(which, head_of(source, k), homes[which], k)
                copy.start()
                arrivals.append((which, k, copy))

    for copy in own_loads:
        copy.wait()
    lane = lax.broadcasted_iota(jnp.int32, (1, LANES), 1)
    ones = jnp.ones((8, d), jnp.float32)
    repeats = LANES // tokens
    for h in range(n_out):
        cut = slice(h * d, (h + 1) * d)
        product = own_g[:, cut].astype(jnp.float32) * own_o[:, cut].astype(jnp.float32)
        product = jnp.concatenate([product] * repeats, axis=0)
        delta = across_rows(ones, product, precision=lax.Precision.HIGHEST)
        stat_send[h, 0:1, :] = l_ref[h : h + 1, :]
        stat_send[h, 1:2, :] = delta[0:1, :]
    for k in range(n_out):
        copy = exchange(4, stat_send.at[other(k)], stat.at[0, o], k)
        copy.start()
        arrivals.append((4, k, copy))

    for copy in text_loads:
        copy.wait()
    for a in range(columns):
        product = qg[a, 1, text].astype(jnp.float32) * text_o[a].astype(jnp.float32)
        delta = across_rows(ones, product, precision=lax.Precision.HIGHEST)
        row_stat[a, 0:1, text] = lt_ref[row_peer(a)]
        row_stat[a, 1:2, text] = delta[0:1, :]

    dq_acc[...] = jnp.zeros_like(dq_acc)
    dkv_acc[...] = jnp.zeros_like(dkv_acc)

    def gather(which, offset):
        group = rows if which < 2 else columns
        place = (group - offset) % group
        if which < 4:
            buffer = (kv, kv, qg, qg)[which]
            source = buffer.at[0, which % 2, pl.ds(0, block)]
            target = buffer.at[place, which % 2, pl.ds(0, block)]
        else:
            source, target = stat.at[0], stat.at[place]
        peer = column_peer(offset) if which < 2 else row_peer(offset)
        return pltpu.make_async_remote_copy(
            src_ref=source,
            dst_ref=target,
            send_sem=gather_send.at[which, offset],
            recv_sem=gather_recv.at[which, place],
            device_id=(o, peer),
            device_id_type=MESH,
        )

    for which in (0, 1, 2, 3, 4):
        for kind, k, copy in arrivals:
            if kind == which:
                if k == 0:
                    copy.wait()
                else:
                    copy.wait_recv()
        for offset in range(1, rows if which < 2 else columns):
            gather(which, offset).start()

    def spread_statistics(a):
        for start in range(0, block, LANES):
            first = start // tokens
            lines = [stat[a, first + p] for p in range(min(repeats, n_out - first))]
            merged = lines[0]
            for p in range(1, len(lines)):
                merged = jnp.where(lane // tokens == p, lines[p], merged)
            row_stat[a, :, start : start + LANES] = merged

    def flip_keys(b):
        key_flip[b] = kv[b, 0].astype(jnp.float32).T.astype(jnp.bfloat16)

    size = math.gcd(block, 256)
    chunks = [(start, size) for start in range(0, block, size)] + [(block, share)]

    def total(kind, offset):
        group = rows if kind else columns
        place = (group - offset) % group
        send, recv = ((dq_send, dq_recv), (dkv_send, dkv_recv))[kind]
        peer = column_peer(offset) if kind else row_peer(offset)
        return pltpu.make_async_remote_copy(
            src_ref=send.at[offset],
            dst_ref=recv.at[place],
            send_sem=sum_send.at[kind, offset],
            recv_sem=sum_recv.at[kind, place],
            device_id=(o, peer),
            device_id_type=MESH,
        )

    def query_sum(a):
        return dq_acc[a].T * scale

    def step(s, carry):
        a = s // rows
        turn = s % rows
        b = jnp.where(a == 0, turn, (turn + 1) % rows)

        @pl.when(a == 0)
        def _():
            @pl.when(b > 0)
            def _():
                gather(0, (rows - b) % rows).wait_recv()
                gather(1, (rows - b) % rows).wait_recv()

            flip_keys(b)

        @pl.when(turn == 0)
        def _():
            @pl.when(a > 0)
            def _():
                for which in (2, 3, 4):
                    gather(which, (columns - a) % columns).wait_recv()

            spread_statistics(a)

        keys, values, flipped = kv[b, 0], kv[b, 1], key_flip[b]
        for start, length in chunks:
            cut = slice(start, start + length)
            queries, upstream = qg[a, 0, cut], qg[a, 1, cut]
            scores = across_rows(keys, queries) * scale
            weights = jnp.exp(scores - row_stat[a, 0:1, cut])
            slopes = across_rows(values, upstream)
            mixed = (weights * (slopes - row_stat[a, 1:2, cut])).astype(jnp.bfloat16)
            weights = weights.astype(jnp.bfloat16)
            dkv_acc[b, 1] += jnp.dot(weights, upstream, preferred_element_type=jnp.float32)
            dkv_acc[b, 0] += jnp.dot(mixed, queries, preferred_element_type=jnp.float32)
            dq_acc[a, :, cut] += jnp.dot(flipped, mixed, preferred_element_type=jnp.float32)

        @pl.when(jnp.logical_and(a == columns - 1, b > 0))
        def _():
            dkv_send[b, 0] = (dkv_acc[b, 0] * scale).astype(jnp.bfloat16)
            dkv_send[b, 1] = dkv_acc[b, 1].astype(jnp.bfloat16)
            total(1, b).start()

        @pl.when(jnp.logical_and(a > 0, turn == rows - 1))
        def _():
            dq_send[a] = query_sum(a).astype(jnp.bfloat16)
            total(0, a).start()

        return carry

    lax.fori_loop(0, rows * columns, step, 0)

    outs = []

    def give_back(which, target):
        mine = pl.ds(pl.multiple_of(o * d, d), d)
        for k in range(n_out):
            piece = final.at[which, pl.ds(pl.multiple_of(other(k) * tokens, tokens), tokens)]
            if k == 0:
                copy = pltpu.make_async_copy(piece, target.at[:, mine], out_recv.at[which, 0])
            else:
                copy = pltpu.make_async_remote_copy(
                    src_ref=piece,
                    dst_ref=target.at[:, mine],
                    send_sem=out_send.at[which, k],
                    recv_sem=out_recv.at[which, k],
                    device_id=(other(k), i),
                    device_id_type=MESH,
                )
            copy.start()
            outs.append((k, copy))

    grad = query_sum(0)
    for a in range(1, columns):
        total(0, (columns - a) % columns).wait_recv()
        grad = grad + dq_recv[a].astype(jnp.float32)
    grad = grad.astype(jnp.bfloat16)
    final[0] = grad
    give_back(0, out_q)
    out_qt[...] = grad[block:]

    for b in range(1, rows):
        total(1, (rows - b) % rows).wait_recv()
    for part, image, own_text in ((0, out_k, out_kt), (1, out_v, out_vt)):
        grad = dkv_acc[0, part]
        if part == 0:
            grad = grad * scale
        for b in range(1, rows):
            grad = grad + dkv_recv[b, part].astype(jnp.float32)
        grad = grad.astype(jnp.bfloat16)
        final[1 + part] = grad
        give_back(1 + part, image)
        own_text[...] = grad[block:]

    for kind, k, copy in arrivals:
        if k > 0:
            copy.wait_send()
    for which in range(5):
        for offset in range(1, rows if which < 2 else columns):
            gather(which, offset).wait_send()
    for a in range(1, columns):
        total(0, a).wait_send()
    for b in range(1, rows):
        total(1, b).wait_send()
    for k, copy in outs:
        copy.wait()


def shards(
    mesh,
    query_image,
    key_image,
    value_image,
    attended_image,
    upstream_image,
    logsum_image,
    query_text,
    key_text,
    value_text,
    attended_text,
    upstream_text,
    logsum_text,
):
    n_out, n_in = mesh.shape["outer"], mesh.shape["inner"]
    columns = max(c for c in range(1, math.isqrt(n_in) + 1) if n_in % c == 0)
    rows = n_in // columns
    tokens, width = query_image.shape
    block = tokens * n_out
    share = query_text.shape[0] // n_in
    span = block + share
    d = HEAD_DIM
    image_lines = jnp.concatenate([logsum_image.T] * (LANES // tokens), axis=1)
    text_lines = logsum_text.reshape(n_in, 1, share)
    half, full = jnp.bfloat16, jnp.float32
    dma = pltpu.SemaphoreType.DMA
    vmem = pl.BlockSpec(memory_space=pltpu.VMEM)
    hbm = pl.BlockSpec(memory_space=pl.ANY)
    image_out = jax.ShapeDtypeStruct((tokens, width), half)
    text_out = jax.ShapeDtypeStruct((share, d), half)
    return pl.pallas_call(
        functools.partial(kernel, (n_out, n_in, rows, columns, tokens, block, share)),
        out_shape=(image_out,) * 3 + (text_out,) * 3,
        in_specs=[hbm] * 5 + [vmem] + [hbm] * 5 + [vmem],
        out_specs=(vmem,) * 6,
        scratch_shapes=[
            pltpu.VMEM((columns, 2, span, d), half),
            pltpu.VMEM((rows, 2, span, d), half),
            pltpu.VMEM((rows, d, span), half),
            pltpu.VMEM((n_out, 2, LANES), full),
            pltpu.VMEM((columns, n_out, 2, LANES), full),
            pltpu.VMEM((columns, 2, span), full),
            pltpu.VMEM((tokens, width), half),
            pltpu.VMEM((tokens, width), half),
            pltpu.VMEM((columns, share, d), half),
            pltpu.VMEM((columns, d, span), full),
            pltpu.VMEM((rows, 2, span, d), full),
            pltpu.VMEM((columns, span, d), half),
            pltpu.VMEM((columns, span, d), half),
            pltpu.VMEM((rows, 2, span, d), half),
            pltpu.VMEM((rows, 2, span, d), half),
            pltpu.VMEM((3, span, d), half),
            dma((2,)),
            dma((2 * rows + 3 * columns,)),
            dma((5, n_out)),
            dma((5, n_out)),
            dma((5, max(rows, columns))),
            dma((5, max(rows, columns))),
            dma((2, max(rows, columns))),
            dma((2, max(rows, columns))),
            dma((3, n_out)),
            dma((3, n_out)),
        ],
        compiler_params=pltpu.CompilerParams(collective_id=0, has_side_effects=True),
    )(
        query_image, key_image, value_image, attended_image, upstream_image, image_lines,
        query_text, key_text, value_text, attended_text, upstream_text, text_lines,
    )


def solution(mesh):
    tokens_spec = P(("outer", "inner"), None)
    return jax.shard_map(
        functools.partial(shards, mesh),
        mesh=mesh,
        in_specs=(tokens_spec,) * 6 + (P(None, "outer"),) * 6,
        out_specs=(tokens_spec,) * 3 + (P("inner", "outer"),) * 3,
        check_vma=False,
    )
```

```python
import functools
import math

import jax
import jax.numpy as jnp
from jax import lax
from jax.experimental import pallas as pl
from jax.experimental.pallas import tpu as pltpu
from jax.sharding import PartitionSpec as P

HEAD_DIM = 128
LANES = 128
MESH = pl.DeviceIdType.MESH


def across_rows(left, right, **options):
    return lax.dot_general(
        left, right, (((1,), (1,)), ((), ())), preferred_element_type=jnp.float32, **options
    )


def kernel(
    dims,
    q_ref, k_ref, v_ref, o_ref, g_ref, l_ref,
    qt_ref, kt_ref, vt_ref, ot_ref, gt_ref, lt_ref,
    out_q, out_k, out_v, out_qt, out_kt, out_vt,
    qg, kv, key_flip, lines_in, stat_send, stat, row_stat, own_o, own_g, text_o,
    dq_acc, dkv_acc, dq_send, dq_recv, dkv_send, dkv_recv, final,
    local_sem, text_sem, in_send, in_recv, gather_send, gather_recv,
    sum_send, sum_recv, out_send, out_recv,
):
    n_out, n_in, rows, columns, tokens, block, share = dims
    span = block + share
    d = HEAD_DIM
    scale = HEAD_DIM ** (-0.5)
    o = lax.axis_index("outer")
    i = lax.axis_index("inner")

    line, place_in = i // rows, i % rows

    def row_peer(a):
        return (line + a) % columns * rows + place_in

    def column_peer(b):
        return line * rows + (place_in + b) % rows

    def other(k):
        return (o + k) % n_out

    own_loads = [
        pltpu.make_async_copy(g_ref, own_g, local_sem.at[0]),
        pltpu.make_async_copy(o_ref, own_o, local_sem.at[1]),
    ]
    for copy in own_loads:
        copy.start()

    barrier = pltpu.get_barrier_semaphore()
    for k in range(1, n_out):
        pl.semaphore_signal(barrier, inc=1, device_id=(other(k), i), device_id_type=MESH)
    for a in range(1, columns):
        pl.semaphore_signal(barrier, inc=1, device_id=(o, row_peer(a)), device_id_type=MESH)
    for b in range(1, rows):
        pl.semaphore_signal(barrier, inc=1, device_id=(o, column_peer(b)), device_id_type=MESH)

    text_loads = []

    def text_load(source, peer, target):
        copy = pltpu.make_async_copy(
            source.at[pl.ds(pl.multiple_of(peer * share, share), share)],
            target,
            text_sem.at[len(text_loads)],
        )
        copy.start()
        text_loads.append(copy)

    text = pl.ds(block, share)
    for b in range(rows):
        text_load(kt_ref, column_peer(b), kv.at[b, 0, text])
        text_load(vt_ref, column_peer(b), kv.at[b, 1, text])
    for a in range(columns):
        text_load(qt_ref, row_peer(a), qg.at[a, 0, text])
        text_load(gt_ref, row_peer(a), qg.at[a, 1, text])
        text_load(ot_ref, row_peer(a), text_o.at[a])

    pl.semaphore_wait(barrier, n_out - 1 + columns - 1 + rows - 1)

    def piece(k):
        return pl.ds(k * tokens, tokens)

    def exchange(which, source, target, k):
        if k == 0:
            return pltpu.make_async_copy(source, target, in_recv.at[which, 0])
        return pltpu.make_async_remote_copy(
            src_ref=source,
            dst_ref=target,
            send_sem=in_send.at[which, k],
            recv_sem=in_recv.at[which, k],
            device_id=(other(k), i),
            device_id_type=MESH,
        )

    def head_of(ref, k):
        return ref.at[:, pl.ds(pl.multiple_of(other(k) * d, d), d)]

    homes = (kv, kv, qg, qg)
    arrivals = {}
    for pair in ((2, 3), (0, 1)):
        for k in range(n_out):
            for which in pair:
                source = (k_ref, v_ref, q_ref, g_ref)[which]
                copy = exchange(which, head_of(source, k), homes[which].at[0, which % 2, piece(k)], k)
                copy.start()
                arrivals[which, k] = copy

    for copy in own_loads:
        copy.wait()
    lane = lax.broadcasted_iota(jnp.int32, (1, LANES), 1)
    ones = jnp.ones((8, d), jnp.float32)
    repeats = LANES // tokens
    lines_in[...] = jnp.zeros_like(lines_in)
    lines_in[:, 0:tokens] = l_ref[...]
    image_lines = lines_in[...]
    for p in range(1, repeats):
        moved = pltpu.roll(lines_in[...], p * tokens, 1)
        image_lines = jnp.where(lane // tokens == p, moved, image_lines)
    for h in range(n_out):
        cut = slice(h * d, (h + 1) * d)
        product = own_g[:, cut].astype(jnp.float32) * own_o[:, cut].astype(jnp.float32)
        product = jnp.concatenate([product] * repeats, axis=0)
        delta = across_rows(ones, product, precision=lax.Precision.HIGHEST)
        stat_send[h, 0:1, :] = image_lines[h : h + 1, :]
        stat_send[h, 1:2, :] = delta[0:1, :]
    for k in range(n_out):
        copy = exchange(4, stat_send.at[other(k)], stat.at[0, k], k)
        copy.start()
        arrivals[4, k] = copy

    for copy in text_loads:
        copy.wait()
    for a in range(columns):
        product = qg[a, 1, text].astype(jnp.float32) * text_o[a].astype(jnp.float32)
        delta = across_rows(ones, product, precision=lax.Precision.HIGHEST)
        row_stat[a, 0:1, text] = lt_ref[row_peer(a)]
        row_stat[a, 1:2, text] = delta[0:1, :]

    def gather(which, offset, k):
        group = rows if which < 2 else columns
        place = (group - offset) % group
        if which < 4:
            source = homes[which].at[0, which % 2, piece(k)]
            target = homes[which].at[place, which % 2, piece(k)]
        else:
            source, target = stat.at[0], stat.at[place]
        peer = column_peer(offset) if which < 2 else row_peer(offset)
        return pltpu.make_async_remote_copy(
            src_ref=source,
            dst_ref=target,
            send_sem=gather_send.at[which, offset, k],
            recv_sem=gather_recv.at[which, place, k],
            device_id=(o, peer),
            device_id_type=MESH,
        )

    def landed(which, k):
        if k == 0:
            arrivals[which, k].wait()
        else:
            arrivals[which, k].wait_recv()

    for k in range(n_out):
        for which in (2, 3):
            landed(which, k)
            for offset in range(1, columns):
                gather(which, offset, k).start()
    for k in range(n_out):
        landed(4, k)
    for offset in range(1, columns):
        gather(4, offset, 0).start()
    for k in range(n_out):
        for which in (0, 1):
            landed(which, k)
            for offset in range(1, rows):
                gather(which, offset, k).start()

    dq_acc[...] = jnp.zeros_like(dq_acc)
    dkv_acc[...] = jnp.zeros_like(dkv_acc)

    def spread_statistics(a):
        for start in range(0, block, LANES):
            first = start // tokens
            lines = [stat[a, first + p] for p in range(min(repeats, n_out - first))]
            merged = lines[0]
            for p in range(1, len(lines)):
                merged = jnp.where(lane // tokens == p, lines[p], merged)
            row_stat[a, :, start : start + LANES] = merged

    def flip_keys(b):
        key_flip[b] = kv[b, 0].astype(jnp.float32).T.astype(jnp.bfloat16)

    size = math.gcd(block, 256)
    chunks = [(start, size) for start in range(0, block, size)] + [(block, share)]
    halves = [(0, size), (size, span - size)]

    def total(kind, offset, n):
        group = rows if kind else columns
        place = (group - offset) % group
        start, length = (halves if kind else chunks)[n]
        cut = pl.ds(start, length)
        if kind:
            source, target = dkv_send.at[offset, kind - 1, cut], dkv_recv.at[place, kind - 1, cut]
        else:
            source, target = dq_send.at[offset, cut], dq_recv.at[place, cut]
        peer = column_peer(offset) if kind else row_peer(offset)
        return pltpu.make_async_remote_copy(
            src_ref=source,
            dst_ref=target,
            send_sem=sum_send.at[kind, offset, n],
            recv_sem=sum_recv.at[kind, place, n],
            device_id=(o, peer),
            device_id_type=MESH,
        )

    def query_sum(a, n):
        start, length = chunks[n]
        return dq_acc[a, :, start : start + length].T * scale

    def work(a, b, n):
        start, length = chunks[n]
        cut = slice(start, start + length)
        keys, values = kv[b, 0], kv[b, 1]
        queries, upstream = qg[a, 0, cut], qg[a, 1, cut]
        scores = across_rows(keys, queries) * scale
        weights = jnp.exp(scores - row_stat[a, 0:1, cut])
        slopes = across_rows(values, upstream)
        mixed = (weights * (slopes - row_stat[a, 1:2, cut])).astype(jnp.bfloat16)
        weights = weights.astype(jnp.bfloat16)
        dkv_acc[b, 1] += jnp.dot(weights, upstream, preferred_element_type=jnp.float32)
        dkv_acc[b, 0] += jnp.dot(mixed, queries, preferred_element_type=jnp.float32)
        dq_acc[a, :, cut] += jnp.dot(key_flip[b], mixed, preferred_element_type=jnp.float32)

    spread_statistics(0)
    flip_keys(0)
    for n in range(len(chunks)):
        work(0, 0, n)

    def near_keys(b, carry):
        for which in (0, 1):
            for k in range(n_out):
                gather(which, (rows - b) % rows, k).wait_recv()
        flip_keys(b)
        for n in range(len(chunks)):
            work(0, b, n)
        return carry

    lax.fori_loop(1, rows, near_keys, 0)

    def far_queries(a, carry):
        offset = (columns - a) % columns
        for n in (len(chunks) - 1, *range(len(chunks) - 1)):
            start, length = chunks[n]
            if start == 0:
                gather(4, offset, 0).wait_recv()
                spread_statistics(a)
            if start < block:
                for k in range(start // tokens, (start + length) // tokens):
                    gather(2, offset, k).wait_recv()
                    gather(3, offset, k).wait_recv()

            def with_keys(b, carry):
                work(a, b, n)
                return carry

            lax.fori_loop(0, rows, with_keys, 0)
            dq_send[a, start : start + length] = query_sum(a, n).astype(jnp.bfloat16)
            total(0, a, n).start()
        return carry

    lax.fori_loop(1, columns, far_queries, 0)

    for b in range(1, rows):
        for part in (0, 1):
            grad = dkv_acc[b, part]
            if part == 0:
                grad = grad * scale
            dkv_send[b, part] = grad.astype(jnp.bfloat16)
            for n in range(len(halves)):
                total(1 + part, b, n).start()

    outs = []
    mine = pl.ds(pl.multiple_of(o * d, d), d)

    def give_back(which, target, text_target, start, length):
        for k in range(start // tokens, min(start + length, block) // tokens):
            source = final.at[which, piece(k)]
            if k == 0:
                copy = pltpu.make_async_copy(source, target.at[:, mine], out_recv.at[which, 0])
            else:
                copy = pltpu.make_async_remote_copy(
                    src_ref=source,
                    dst_ref=target.at[:, mine],
                    send_sem=out_send.at[which, k],
                    recv_sem=out_recv.at[which, k],
                    device_id=((o + n_out - k) % n_out, i),
                    device_id_type=MESH,
                )
            copy.start()
            outs.append(copy)
        if start + length == span:
            copy = pltpu.make_async_copy(final.at[which, text], text_target, out_send.at[which, 0])
            copy.start()
            outs.append(copy)

    for n in (len(chunks) - 1, *range(len(chunks) - 1)):
        start, length = chunks[n]
        cut = slice(start, start + length)
        grad = query_sum(0, n)
        for a in range(1, columns):
            total(0, (columns - a) % columns, n).wait_recv()
            grad = grad + dq_recv[a, cut].astype(jnp.float32)
        final[0, cut] = grad.astype(jnp.bfloat16)
        give_back(0, out_q, out_qt, start, length)

    for part, image, own_text in ((0, out_k, out_kt), (1, out_v, out_vt)):
        for n, (start, length) in enumerate(halves):
            cut = slice(start, start + length)
            grad = dkv_acc[0, part, cut]
            if part == 0:
                grad = grad * scale
            for b in range(1, rows):
                total(1 + part, (rows - b) % rows, n).wait_recv()
                grad = grad + dkv_recv[b, part, cut].astype(jnp.float32)
            final[1 + part, cut] = grad.astype(jnp.bfloat16)
            give_back(1 + part, image, own_text, start, length)

    for (which, k), copy in arrivals.items():
        if k > 0:
            copy.wait_send()
    for which in range(4):
        for offset in range(1, rows if which < 2 else columns):
            for k in range(n_out):
                gather(which, offset, k).wait_send()
    for a in range(1, columns):
        gather(4, a, 0).wait_send()
        for n in range(len(chunks)):
            total(0, a, n).wait_send()
    for b in range(1, rows):
        for n in range(len(halves)):
            total(1, b, n).wait_send()
            total(2, b, n).wait_send()
    for copy in outs:
        copy.wait()


def tail(*refs):
    sources, targets, held = refs[:6], refs[6:12], refs[12:18]
    sem = refs[18]
    loads = [pltpu.make_async_copy(s, h, sem.at[0, n]) for n, (s, h) in enumerate(zip(sources, held))]
    stores = [pltpu.make_async_copy(h, t, sem.at[1, n]) for n, (h, t) in enumerate(zip(held, targets))]
    for load in loads:
        load.start()
    for load, store in zip(loads, stores):
        load.wait()
        store.start()
    for store in stores:
        store.wait()


def shards(
    mesh,
    query_image,
    key_image,
    value_image,
    attended_image,
    upstream_image,
    logsum_image,
    query_text,
    key_text,
    value_text,
    attended_text,
    upstream_text,
    logsum_text,
):
    n_out, n_in = mesh.shape["outer"], mesh.shape["inner"]
    rows = max(c for c in range(1, math.isqrt(n_in) + 1) if n_in % c == 0)
    columns = n_in // rows
    tokens, width = query_image.shape
    block = tokens * n_out
    share = query_text.shape[0] // n_in
    span = block + share
    d = HEAD_DIM
    text_lines = logsum_text.reshape(n_in, 1, share)
    half, full = jnp.bfloat16, jnp.float32
    dma = pltpu.SemaphoreType.DMA
    vmem = pl.BlockSpec(memory_space=pltpu.VMEM)
    hbm = pl.BlockSpec(memory_space=pl.ANY)
    image_out = jax.ShapeDtypeStruct((tokens, width), half)
    text_out = jax.ShapeDtypeStruct((share, d), half)
    grads = pl.pallas_call(
        functools.partial(kernel, (n_out, n_in, rows, columns, tokens, block, share)),
        out_shape=(image_out,) * 3 + (text_out,) * 3,
        in_specs=[hbm] * 5 + [vmem] + [hbm] * 5 + [vmem],
        out_specs=(hbm,) * 6,
        scratch_shapes=[
            pltpu.VMEM((columns, 2, span, d), half),
            pltpu.VMEM((rows, 2, span, d), half),
            pltpu.VMEM((rows, d, span), half),
            pltpu.VMEM((n_out, LANES), full),
            pltpu.VMEM((n_out, 2, LANES), full),
            pltpu.VMEM((columns, n_out, 2, LANES), full),
            pltpu.VMEM((columns, 2, span), full),
            pltpu.VMEM((tokens, width), half),
            pltpu.VMEM((tokens, width), half),
            pltpu.VMEM((columns, share, d), half),
            pltpu.VMEM((columns, d, span), full),
            pltpu.VMEM((rows, 2, span, d), full),
            pltpu.VMEM((columns, span, d), half),
            pltpu.VMEM((columns, span, d), half),
            pltpu.VMEM((rows, 2, span, d), half),
            pltpu.VMEM((rows, 2, span, d), half),
            pltpu.VMEM((3, span, d), half),
            dma((2,)),
            dma((2 * rows + 3 * columns,)),
            dma((5, n_out)),
            dma((5, n_out)),
            dma((5, max(rows, columns), n_out)),
            dma((5, max(rows, columns), n_out)),
            dma((3, max(rows, columns), 1 + block // math.gcd(block, 256))),
            dma((3, max(rows, columns), 1 + block // math.gcd(block, 256))),
            dma((3, n_out)),
            dma((3, n_out)),
        ],
        compiler_params=pltpu.CompilerParams(collective_id=0, has_side_effects=True),
    )(
        query_image, key_image, value_image, attended_image, upstream_image, logsum_image.T,
        query_text, key_text, value_text, attended_text, upstream_text, text_lines,
    )
    return pl.pallas_call(
        tail,
        out_shape=(image_out,) * 3 + (text_out,) * 3,
        in_specs=[hbm] * 6,
        out_specs=(hbm,) * 6,
        scratch_shapes=[pltpu.VMEM((tokens, width), half)] * 3
        + [pltpu.VMEM((share, d), half)] * 3
        + [dma((2, 6))],
    )(*grads)


def solution(mesh):
    tokens_spec = P(("outer", "inner"), None)
    return jax.shard_map(
        functools.partial(shards, mesh),
        mesh=mesh,
        in_specs=(tokens_spec,) * 6 + (P(None, "outer"),) * 6,
        out_specs=(tokens_spec,) * 3 + (P("inner", "outer"),) * 3,
        check_vma=False,
    )
```

```python
import functools
import math

import jax
import jax.numpy as jnp
from jax import lax
from jax.experimental import pallas as pl
from jax.experimental.pallas import tpu as pltpu
from jax.sharding import PartitionSpec as P

HEAD_DIM = 128
LANES = 128
MESH = pl.DeviceIdType.MESH


def across_rows(left, right, **options):
    return lax.dot_general(
        left, right, (((1,), (1,)), ((), ())), preferred_element_type=jnp.float32, **options
    )


def kernel(
    dims,
    q_ref, k_ref, v_ref, o_ref, g_ref, l_ref,
    qt_ref, kt_ref, vt_ref, ot_ref, gt_ref, lt_ref,
    out_q, out_k, out_v, out_qt, out_kt, out_vt,
    qg, kv, key_flip, lines_in, stat_send, stat, row_stat, own_o, own_g, text_o,
    dq_acc, dkv_acc, dq_send, dq_recv, dkv_send, dkv_recv, final,
    local_sem, text_sem, in_send, in_recv, gather_send, gather_recv,
    sum_send, sum_recv, out_send, out_recv,
):
    n_out, n_in, rows, columns, tokens, block, share = dims
    span = block + share
    d = HEAD_DIM
    scale = HEAD_DIM ** (-0.5)
    o = lax.axis_index("outer")
    i = lax.axis_index("inner")

    line, place_in = i // rows, i % rows

    def row_peer(a):
        return (line + a) % columns * rows + place_in

    def column_peer(b):
        return line * rows + (place_in + b) % rows

    def other(k):
        return (o + k) % n_out

    own_loads = [
        pltpu.make_async_copy(g_ref, own_g, local_sem.at[0]),
        pltpu.make_async_copy(o_ref, own_o, local_sem.at[1]),
    ]
    for copy in own_loads:
        copy.start()

    barrier = pltpu.get_barrier_semaphore()
    for k in range(1, n_out):
        pl.semaphore_signal(barrier, inc=1, device_id=(other(k), i), device_id_type=MESH)
    for a in range(1, columns):
        pl.semaphore_signal(barrier, inc=1, device_id=(o, row_peer(a)), device_id_type=MESH)
    for b in range(1, rows):
        pl.semaphore_signal(barrier, inc=1, device_id=(o, column_peer(b)), device_id_type=MESH)

    text_loads = []

    def text_load(source, peer, target):
        copy = pltpu.make_async_copy(
            source.at[pl.ds(pl.multiple_of(peer * share, share), share)],
            target,
            text_sem.at[len(text_loads)],
        )
        copy.start()
        text_loads.append(copy)

    text = pl.ds(block, share)
    for b in range(rows):
        text_load(kt_ref, column_peer(b), kv.at[b, 0, text])
        text_load(vt_ref, column_peer(b), kv.at[b, 1, text])
    for a in range(columns):
        text_load(qt_ref, row_peer(a), qg.at[a, 0, text])
        text_load(gt_ref, row_peer(a), qg.at[a, 1, text])
        text_load(ot_ref, row_peer(a), text_o.at[a])

    pl.semaphore_wait(barrier, n_out - 1 + columns - 1 + rows - 1)

    def piece(k):
        return pl.ds(k * tokens, tokens)

    def exchange(which, source, target, k):
        if k == 0:
            return pltpu.make_async_copy(source, target, in_recv.at[which, 0])
        return pltpu.make_async_remote_copy(
            src_ref=source,
            dst_ref=target,
            send_sem=in_send.at[which, k],
            recv_sem=in_recv.at[which, k],
            device_id=(other(k), i),
            device_id_type=MESH,
        )

    def head_of(ref, k):
        return ref.at[:, pl.ds(pl.multiple_of(other(k) * d, d), d)]

    homes = (kv, kv, qg, qg)

    def arrival(which, k):
        if which == 4:
            return exchange(4, stat_send.at[other(k)], stat.at[0, k], k)
        source = (k_ref, v_ref, q_ref, g_ref)[which]
        return exchange(which, head_of(source, k), homes[which].at[0, which % 2, piece(k)], k)

    at_end = jnp.logical_or(i == 0, i == n_in - 1)

    def ordered(first, second):
        @pl.when(at_end)
        def _():
            first()
            second()

        @pl.when(jnp.logical_not(at_end))
        def _():
            second()
            first()

    def depart(pair):
        for k in range(n_out):
            for which in pair:
                arrival(which, k).start()

    ordered(lambda: depart((0, 1)), lambda: depart((2, 3)))

    for copy in own_loads:
        copy.wait()
    lane = lax.broadcasted_iota(jnp.int32, (1, LANES), 1)
    ones = jnp.ones((8, d), jnp.float32)
    repeats = LANES // tokens
    lines_in[...] = jnp.zeros_like(lines_in)
    lines_in[:, 0:tokens] = l_ref[...]
    image_lines = lines_in[...]
    for p in range(1, repeats):
        moved = pltpu.roll(lines_in[...], p * tokens, 1)
        image_lines = jnp.where(lane // tokens == p, moved, image_lines)
    for h in range(n_out):
        cut = slice(h * d, (h + 1) * d)
        product = own_g[:, cut].astype(jnp.float32) * own_o[:, cut].astype(jnp.float32)
        product = jnp.concatenate([product] * repeats, axis=0)
        delta = across_rows(ones, product, precision=lax.Precision.HIGHEST)
        stat_send[h, 0:1, :] = image_lines[h : h + 1, :]
        stat_send[h, 1:2, :] = delta[0:1, :]
    for k in range(n_out):
        arrival(4, k).start()

    for copy in text_loads:
        copy.wait()
    for a in range(columns):
        product = qg[a, 1, text].astype(jnp.float32) * text_o[a].astype(jnp.float32)
        delta = across_rows(ones, product, precision=lax.Precision.HIGHEST)
        row_stat[a, 0:1, text] = lt_ref[row_peer(a)]
        row_stat[a, 1:2, text] = delta[0:1, :]

    def gather(which, offset, k):
        group = rows if which < 2 else columns
        place = (group - offset) % group
        if which < 4:
            source = homes[which].at[0, which % 2, piece(k)]
            target = homes[which].at[place, which % 2, piece(k)]
        else:
            source, target = stat.at[0], stat.at[place]
        peer = column_peer(offset) if which < 2 else row_peer(offset)
        return pltpu.make_async_remote_copy(
            src_ref=source,
            dst_ref=target,
            send_sem=gather_send.at[which, offset, k],
            recv_sem=gather_recv.at[which, place, k],
            device_id=(o, peer),
            device_id_type=MESH,
        )

    def landed(which, k):
        if k == 0:
            arrival(which, k).wait()
        else:
            arrival(which, k).wait_recv()

    def forward(pair, group):
        for k in range(n_out):
            for which in pair:
                landed(which, k)
                for offset in range(1, group):
                    gather(which, offset, k).start()

    ordered(lambda: forward((0, 1), rows), lambda: forward((2, 3), columns))
    for k in range(n_out):
        landed(4, k)
    for offset in range(1, columns):
        gather(4, offset, 0).start()

    dq_acc[...] = jnp.zeros_like(dq_acc)
    dkv_acc[...] = jnp.zeros_like(dkv_acc)

    def spread_statistics(a):
        for start in range(0, block, LANES):
            first = start // tokens
            lines = [stat[a, first + p] for p in range(min(repeats, n_out - first))]
            merged = lines[0]
            for p in range(1, len(lines)):
                merged = jnp.where(lane // tokens == p, lines[p], merged)
            row_stat[a, :, start : start + LANES] = merged

    def flip_keys(b):
        key_flip[b] = kv[b, 0].astype(jnp.float32).T.astype(jnp.bfloat16)

    size = math.gcd(block, 256)
    chunks = [(start, size) for start in range(0, block, size)] + [(block, share)]
    halves = [(0, size), (size, span - size)]

    def total(kind, offset, n):
        group = rows if kind else columns
        place = (group - offset) % group
        start, length = (halves if kind else chunks)[n]
        cut = pl.ds(start, length)
        if kind:
            source, target = dkv_send.at[offset, kind - 1, cut], dkv_recv.at[place, kind - 1, cut]
        else:
            source, target = dq_send.at[offset, cut], dq_recv.at[place, cut]
        peer = column_peer(offset) if kind else row_peer(offset)
        return pltpu.make_async_remote_copy(
            src_ref=source,
            dst_ref=target,
            send_sem=sum_send.at[kind, offset, n],
            recv_sem=sum_recv.at[kind, place, n],
            device_id=(o, peer),
            device_id_type=MESH,
        )

    def query_sum(a, n):
        start, length = chunks[n]
        return dq_acc[a, :, start : start + length].T * scale

    def work(a, b, n):
        start, length = chunks[n]
        cut = slice(start, start + length)
        keys, values = kv[b, 0], kv[b, 1]
        queries, upstream = qg[a, 0, cut], qg[a, 1, cut]
        scores = across_rows(keys, queries) * scale
        weights = jnp.exp(scores - row_stat[a, 0:1, cut])
        slopes = across_rows(values, upstream)
        mixed = (weights * (slopes - row_stat[a, 1:2, cut])).astype(jnp.bfloat16)
        weights = weights.astype(jnp.bfloat16)
        dkv_acc[b, 1] += jnp.dot(weights, upstream, preferred_element_type=jnp.float32)
        dkv_acc[b, 0] += jnp.dot(mixed, queries, preferred_element_type=jnp.float32)
        dq_acc[a, :, cut] += jnp.dot(key_flip[b], mixed, preferred_element_type=jnp.float32)

    spread_statistics(0)
    flip_keys(0)
    for n in range(len(chunks)):
        work(0, 0, n)

    def near_keys_landed(b):
        for which in (0, 1):
            for k in range(n_out):
                gather(which, (rows - b) % rows, k).wait_recv()
        flip_keys(b)

    def far_queries_landed(a, n):
        start, length = chunks[n]
        if start < block:
            for k in range(start // tokens, (start + length) // tokens):
                gather(2, (columns - a) % columns, k).wait_recv()
                gather(3, (columns - a) % columns, k).wait_recv()
        if start == 0:
            gather(4, (columns - a) % columns, 0).wait_recv()
            spread_statistics(a)

    def send_queries(a, n):
        start, length = chunks[n]
        dq_send[a, start : start + length] = query_sum(a, n).astype(jnp.bfloat16)
        total(0, a, n).start()

    def send_keys(b):
        for part in (0, 1):
            for n, (start, length) in enumerate(halves):
                cut = slice(start, start + length)
                grad = dkv_acc[b, part, cut]
                if part == 0:
                    grad = grad * scale
                dkv_send[b, part, cut] = grad.astype(jnp.bfloat16)
                total(1 + part, b, n).start()

    places = (len(chunks) - 1, *range(len(chunks) - 1))

    def loop(first, last, body):
        def with_carry(index, carry):
            body(index)
            return carry

        lax.fori_loop(first, last, with_carry, 0)

    @pl.when(jnp.logical_not(at_end))
    def _():
        def near_keys(b):
            near_keys_landed(b)
            for n in places:
                work(0, b, n)

        def far_queries(a):
            for n in places:
                far_queries_landed(a, n)
                loop(0, rows, lambda b: work(a, b, n))
                send_queries(a, n)

        loop(1, rows, near_keys)
        loop(1, columns, far_queries)
        loop(1, rows, send_keys)

    @pl.when(at_end)
    def _():
        def far_queries(a):
            for n in places:
                far_queries_landed(a, n)
                work(a, 0, n)

        def near_keys(b):
            near_keys_landed(b)

            def with_queries(a):
                for n in places:
                    work(a, b, n)

            loop(0, columns, with_queries)
            send_keys(b)

        def give_queries(a):
            for n in places:
                send_queries(a, n)

        loop(1, columns, far_queries)
        loop(1, rows, near_keys)
        loop(1, columns, give_queries)

    mine = pl.ds(pl.multiple_of(o * d, d), d)
    images, texts = (out_q, out_k, out_v), (out_qt, out_kt, out_vt)

    def out_copy(which, k):
        source, target = final.at[which, piece(k)], images[which].at[:, mine]
        if k == 0:
            return pltpu.make_async_copy(source, target, out_recv.at[which, 0])
        return pltpu.make_async_remote_copy(
            src_ref=source,
            dst_ref=target,
            send_sem=out_send.at[which, k],
            recv_sem=out_recv.at[which, k],
            device_id=((o + n_out - k) % n_out, i),
            device_id_type=MESH,
        )

    def text_copy(which):
        return pltpu.make_async_copy(final.at[which, text], texts[which], out_send.at[which, 0])

    def give_back(which, start, length):
        for k in range(start // tokens, min(start + length, block) // tokens):
            out_copy(which, k).start()
        if start + length == span:
            text_copy(which).start()

    def finish_queries():
        for n in places:
            start, length = chunks[n]
            cut = slice(start, start + length)
            grad = query_sum(0, n)
            for a in range(1, columns):
                total(0, (columns - a) % columns, n).wait_recv()
                grad = grad + dq_recv[a, cut].astype(jnp.float32)
            final[0, cut] = grad.astype(jnp.bfloat16)
            give_back(0, start, length)

    def finish_keys():
        for part in (0, 1):
            for n, (start, length) in enumerate(halves):
                cut = slice(start, start + length)
                grad = dkv_acc[0, part, cut]
                if part == 0:
                    grad = grad * scale
                for b in range(1, rows):
                    total(1 + part, (rows - b) % rows, n).wait_recv()
                    grad = grad + dkv_recv[b, part, cut].astype(jnp.float32)
                final[1 + part, cut] = grad.astype(jnp.bfloat16)
                give_back(1 + part, start, length)

    ordered(finish_queries, finish_keys)

    for which in range(5):
        for k in range(1, n_out):
            arrival(which, k).wait_send()
    for which in range(4):
        for offset in range(1, rows if which < 2 else columns):
            for k in range(n_out):
                gather(which, offset, k).wait_send()
    for a in range(1, columns):
        gather(4, a, 0).wait_send()
        for n in range(len(chunks)):
            total(0, a, n).wait_send()
    for b in range(1, rows):
        for n in range(len(halves)):
            total(1, b, n).wait_send()
            total(2, b, n).wait_send()
    for which in range(3):
        text_copy(which).wait()
        for k in range(n_out):
            out_copy(which, k).wait()


def tail(*refs):
    sources, targets, held = refs[:6], refs[6:12], refs[12:18]
    sem = refs[18]
    loads = [pltpu.make_async_copy(s, h, sem.at[0, n]) for n, (s, h) in enumerate(zip(sources, held))]
    stores = [pltpu.make_async_copy(h, t, sem.at[1, n]) for n, (h, t) in enumerate(zip(held, targets))]
    for load in loads:
        load.start()
    for load, store in zip(loads, stores):
        load.wait()
        store.start()
    for store in stores:
        store.wait()


def shards(
    mesh,
    query_image,
    key_image,
    value_image,
    attended_image,
    upstream_image,
    logsum_image,
    query_text,
    key_text,
    value_text,
    attended_text,
    upstream_text,
    logsum_text,
):
    n_out, n_in = mesh.shape["outer"], mesh.shape["inner"]
    rows = max(c for c in range(1, math.isqrt(n_in) + 1) if n_in % c == 0)
    columns = n_in // rows
    tokens, width = query_image.shape
    block = tokens * n_out
    share = query_text.shape[0] // n_in
    span = block + share
    d = HEAD_DIM
    text_lines = logsum_text.reshape(n_in, 1, share)
    half, full = jnp.bfloat16, jnp.float32
    dma = pltpu.SemaphoreType.DMA
    vmem = pl.BlockSpec(memory_space=pltpu.VMEM)
    hbm = pl.BlockSpec(memory_space=pl.ANY)
    image_out = jax.ShapeDtypeStruct((tokens, width), half)
    text_out = jax.ShapeDtypeStruct((share, d), half)
    grads = pl.pallas_call(
        functools.partial(kernel, (n_out, n_in, rows, columns, tokens, block, share)),
        out_shape=(image_out,) * 3 + (text_out,) * 3,
        in_specs=[hbm] * 5 + [vmem] + [hbm] * 5 + [vmem],
        out_specs=(hbm,) * 6,
        scratch_shapes=[
            pltpu.VMEM((columns, 2, span, d), half),
            pltpu.VMEM((rows, 2, span, d), half),
            pltpu.VMEM((rows, d, span), half),
            pltpu.VMEM((n_out, LANES), full),
            pltpu.VMEM((n_out, 2, LANES), full),
            pltpu.VMEM((columns, n_out, 2, LANES), full),
            pltpu.VMEM((columns, 2, span), full),
            pltpu.VMEM((tokens, width), half),
            pltpu.VMEM((tokens, width), half),
            pltpu.VMEM((columns, share, d), half),
            pltpu.VMEM((columns, d, span), full),
            pltpu.VMEM((rows, 2, span, d), full),
            pltpu.VMEM((columns, span, d), half),
            pltpu.VMEM((columns, span, d), half),
            pltpu.VMEM((rows, 2, span, d), half),
            pltpu.VMEM((rows, 2, span, d), half),
            pltpu.VMEM((3, span, d), half),
            dma((2,)),
            dma((2 * rows + 3 * columns,)),
            dma((5, n_out)),
            dma((5, n_out)),
            dma((5, max(rows, columns), n_out)),
            dma((5, max(rows, columns), n_out)),
            dma((3, max(rows, columns), 1 + block // math.gcd(block, 256))),
            dma((3, max(rows, columns), 1 + block // math.gcd(block, 256))),
            dma((3, n_out)),
            dma((3, n_out)),
        ],
        compiler_params=pltpu.CompilerParams(collective_id=0, has_side_effects=True),
    )(
        query_image, key_image, value_image, attended_image, upstream_image, logsum_image.T,
        query_text, key_text, value_text, attended_text, upstream_text, text_lines,
    )
    return pl.pallas_call(
        tail,
        out_shape=(image_out,) * 3 + (text_out,) * 3,
        in_specs=[hbm] * 6,
        out_specs=(hbm,) * 6,
        scratch_shapes=[pltpu.VMEM((tokens, width), half)] * 3
        + [pltpu.VMEM((share, d), half)] * 3
        + [dma((2, 6))],
    )(*grads)


def solution(mesh):
    tokens_spec = P(("outer", "inner"), None)
    return jax.shard_map(
        functools.partial(shards, mesh),
        mesh=mesh,
        in_specs=(tokens_spec,) * 6 + (P(None, "outer"),) * 6,
        out_specs=(tokens_spec,) * 3 + (P("inner", "outer"),) * 3,
        check_vma=False,
    )
```
